256 devices in a mesh: row: 8 (over x, y_lo), col: 32 (over y_hi, z, core).
Axes of the slice: x: 4, y: 4 (y_hi: 2, y_lo: 2; y = y_hi * 2 + y_lo), z: 8, core: 2. Of those that a mesh axis runs over, the one named last changes fastest.
Arguments:
- corner: float32 [18432, 18432], P('row', 'col'), may hold values from -0.046875 to 0.046875
- right_proj: float32 [18432, 512], P('col', 'row'), may hold values from -1.5 to 1.5
- left_proj: float32 [18432, 512], P('row', 'col'), may hold values from -1.5 to 1.5
- upstream: float32 [512, 512], replicated, may hold values from -0.25 to 0.25
Outputs:
- corner_right: float32 [18432, 512], P(('row', 'col'))
- corner_left: float32 [18432, 512], P(('col', 'row'))
- right_grad: float32 [18432, 512], P(('col', 'row'))
- left_grad: float32 [18432, 512], P(('row', 'col'))
- corner_grad: float32 [18432, 18432], P('row', 'col')
The draws below stay inside these ranges and needn't reach their ends.
All inputs are finite; a program needn't handle non-finite values.
Results may differ from the reference program's by a relative error of at most 0.00007.
Values sent between devices are 32-bit elements; how exact they have to be, the bound alone decides.
No kernel may reach another device: no remote copies, remote signals or barrier semaphores. Data moves between devices by JAX's collectives and lax.ppermute only.
A program may use at most 64 MiB of HBM per device.

```python
import jax
import jax.numpy as jnp
from jax import lax

ORDER = 18432
CHI = 512


def shard_levels(stream_key, dims, cuts, smallest, high):
    loudness, own = 1.0, jax.random.fold_in(stream_key, 6)
    for axis_at, parts in cuts:
        draws = jnp.exp(jax.random.uniform(jax.random.fold_in(own, axis_at), (parts,), jnp.float32, smallest / len(cuts), high / len(cuts)))
        loudness = loudness * jnp.repeat(draws, dims[axis_at] // parts).reshape([-1 if axis == axis_at else 1 for axis in range(len(dims))])
    return loudness


def gaussian(key, extent, scale, bound, cuts=(), dtype=jnp.bfloat16):
    entries = jax.random.normal(key, extent, jnp.float32) * scale
    if len(cuts) > 0:
        entries = shard_levels(key, extent, cuts, -0.22, 0.18) * entries
    return jnp.clip(entries, min=-bound, max=bound).astype(dtype)


def setup_inputs(seed: int = 0) -> dict:
    arg_keys = jax.random.split(jax.random.key(seed), 5)
    corner = gaussian(arg_keys[0], (ORDER, ORDER), ORDER ** -0.5, 0.046875, ((0, 8), (1, 32)), jnp.float32)
    right_proj = gaussian(arg_keys[1], (ORDER, CHI), 0.25, 1.5, ((0, 32), (1, 8)), jnp.float32)
    left_proj = gaussian(arg_keys[2], (ORDER, CHI), 0.25, 1.5, ((0, 8), (1, 32)), jnp.float32)
    upstream = gaussian(arg_keys[3], (CHI, CHI), CHI ** -0.5, 0.25, (), jnp.float32)
    return {"corner": corner, "right_proj": right_proj, "left_proj": left_proj, "upstream": upstream}


def reference(corner, right_proj, left_proj, upstream):
    best = lax.Precision.HIGHEST
    corner_right = jnp.dot(corner, right_proj, precision=best, preferred_element_type=jnp.float32)
    corner_left = jnp.dot(corner.T, left_proj, precision=best, preferred_element_type=jnp.float32)
    weighted = jnp.dot(left_proj, upstream, precision=best, preferred_element_type=jnp.float32)
    corner_grad = jnp.dot(weighted, right_proj.T, precision=best, preferred_element_type=jnp.float32)
    right_grad = jnp.dot(corner_left, upstream, precision=best, preferred_element_type=jnp.float32)
    left_grad = jnp.dot(corner_right, upstream.T, precision=best, preferred_element_type=jnp.float32)
    return corner_right, corner_left, right_grad, left_grad, corner_grad
```

```python
import jax
import jax.numpy as jnp
from jax import lax
from jax.experimental import pallas as pl
from jax.experimental.pallas import tpu as pltpu
from jax.sharding import Mesh
from jax.sharding import PartitionSpec as P

ROW = ("x", "yl")
COL = ("yh", "z", "core")
STEPS = (0, 1, -1, 2, -2, 3, -3, 4)
F32, BF16 = jnp.float32, jnp.bfloat16


def swapped(value, axis):
    return lax.ppermute(value, axis, [(0, 1), (1, 0)])


def even_pairs(value):
    n = lax.axis_size("z")
    return lax.ppermute(value, "z", [(i, i ^ 1) for i in range(n)])


def odd_pairs(value):
    n = lax.axis_size("z")
    return lax.ppermute(value, "z", [(i, (i + 1) % n if i % 2 else (i - 1) % n) for i in range(n)])


def halves(value):
    high = value.astype(BF16)
    return high, (value - high.astype(F32)).astype(BF16)


def product(a, b, ca, cb):
    dims = (((ca,), (cb,)), ((), ()))

    def one(i, j):
        return lax.dot_general(a[i], b[j], dims, preferred_element_type=F32)

    return one(0, 0) + (one(0, 1) + one(1, 0))


def call(kernel, name, grid, in_specs, out_specs, out_shape, scratch=(), prefetch=0, flops=0):
    return pl.pallas_call(
        kernel,
        name=name,
        grid_spec=pltpu.PrefetchScalarGridSpec(
            num_scalar_prefetch=prefetch,
            grid=grid,
            in_specs=in_specs,
            out_specs=out_specs,
            scratch_shapes=list(scratch),
        ),
        out_shape=out_shape,
        compiler_params=pltpu.CompilerParams(vmem_limit_bytes=48 * 2**20),
        cost_estimate=pl.CostEstimate(flops=flops, transcendentals=0, bytes_accessed=8 * 2**20),
    )


def whole(shape):
    return pl.BlockSpec(shape, lambda *_: (0,) * len(shape))


def turned(corner_t):
    k, n = corner_t.shape
    step = 256

    def kernel(src, high, low):
        high[...], low[...] = halves(src[...].T)

    out = pl.BlockSpec((step, k), lambda i: (i, 0))
    shape = jax.ShapeDtypeStruct((n, k), BF16)
    return call(
        kernel, "turned", (n // step,),
        [pl.BlockSpec((k, step), lambda i: (0, i))], [out, out], [shape, shape],
        flops=2 * n * k,
    )(corner_t)


def row_products(where, high, low, right):
    k = high.shape[1]
    chi = right.shape[0] * right.shape[1]
    zs, rows, parts = 8, 72, 2
    block = zs * 2 * rows // parts

    def kernel(where, high, low, right, keep, give, u_high, u_low, acc):
        @pl.when(pl.program_id(0) == 0)
        def _():
            u_high[...], u_low[...] = halves(right[...].reshape(chi, k))

        acc[...] = product((high[...], low[...]), (u_high[...], u_low[...]), 1, 1)
        core = where[1]
        for i in range(zs // parts):
            keep[i] = acc[pl.ds(pl.multiple_of((2 * i + core) * rows, 8), rows), :]
            give[i] = acc[pl.ds(pl.multiple_of((2 * i + 1 - core) * rows, 8), rows), :]

    spec = pl.BlockSpec((block, k), lambda i, w: (w[0] * parts + i, 0))
    out = pl.BlockSpec((zs // parts, rows, chi), lambda i, w: (i, 0, 0))
    shape = jax.ShapeDtypeStruct((zs, rows, chi), F32)
    return call(
        kernel, "row_products", (parts,),
        [spec, spec, whole(right.shape)], [out, out], [shape, shape],
        [pltpu.VMEM((chi, k), BF16), pltpu.VMEM((chi, k), BF16), pltpu.VMEM((block, chi), F32)],
        prefetch=1, flops=6 * zs * 2 * rows * k * chi,
    )(where, high, low, right)


def column_products(order, corner_t, pieces):
    m, k = corner_t.shape
    wide = pieces[0].shape[0]
    chi = wide * len(pieces)
    step = 768

    def kernel(order, src, *refs):
        pieces, (out, high, low) = refs[: len(refs) - 3], refs[len(refs) - 3 :]
        for i, piece in enumerate(pieces):
            at = pl.ds(pl.multiple_of(order[i] * wide, wide), wide)
            high[at, :], low[at, :] = halves(piece[...])
        part = product(halves(src[...]), (high[...], low[...]), 1, 1)

        @pl.when(pl.program_id(0) == 0)
        def _():
            out[...] = part

        @pl.when(pl.program_id(0) > 0)
        def _():
            out[...] += part

    spec = pl.BlockSpec((wide, step), lambda i, w: (0, i))
    placed = pl.BlockSpec((chi, step), lambda i, w: (0, i))
    shape = jax.ShapeDtypeStruct((chi, k), BF16)
    return call(
        kernel, "column_products", (k // step,),
        [pl.BlockSpec((m, step), lambda i, w: (0, i))] + [spec] * len(pieces),
        [whole((m, chi)), placed, placed],
        [jax.ShapeDtypeStruct((m, chi), F32), shape, shape],
        prefetch=1, flops=6 * m * k * chi,
    )(order, corner_t, *pieces)


def corner_gradient(right, upstream, high, low):
    k = right.shape[2]
    chi, n = high.shape
    step = 768

    def kernel(right, upstream, high, low, out, z_high, z_low):
        @pl.when(pl.program_id(0) == 0)
        def _():
            mixed = product(halves(upstream[...]), halves(right[...].reshape(chi, k)), 1, 0)
            z_high[...], z_low[...] = halves(mixed.T)

        out[...] = product((z_high[...], z_low[...]), (high[...], low[...]), 1, 0)

    placed = pl.BlockSpec((chi, step), lambda i: (0, i))
    return call(
        kernel, "corner_gradient", (n // step,),
        [whole(right.shape), whole(upstream.shape), placed, placed],
        pl.BlockSpec((k, step), lambda i: (0, i)),
        jax.ShapeDtypeStruct((k, n), F32),
        [pltpu.VMEM((k, chi), BF16), pltpu.VMEM((k, chi), BF16)],
        flops=6 * k * n * chi,
    )(right, upstream, high, low)


def total_and_product(parts, upstream, contracted, name):
    shape = parts[0].shape[-2:]

    def kernel(*refs):
        parts, (upstream, total, out) = refs[:-3], refs[-3:]
        found = [part[...] if len(part.shape) == 2 else jnp.sum(part[...], axis=0) for part in parts]
        value = sum(found[1:], found[0])
        total[...] = value
        out[...] = product(halves(value), halves(upstream[...]), 1, contracted)

    out = jax.ShapeDtypeStruct(shape, F32)
    return call(
        kernel, name, (1,), [whole(p.shape) for p in parts] + [whole(upstream.shape)],
        [whole(shape), whole(shape)], [out, out], flops=6 * shape[0] * shape[1] * shape[1],
    )(*parts, upstream)


def body(corner, right_proj, left_proj, upstream):
    corner_t = corner.T
    left = left_proj.T
    right = right_proj.T
    z = lax.axis_index("z")
    core = lax.axis_index("core")
    yh = lax.axis_index("yh")
    sign = 1 - 2 * (z % 2)
    line = lax.axis_size("x") * lax.axis_size("yl")

    copies = jnp.broadcast_to(right, (line, *right.shape))
    right_full = lax.all_to_all(copies, ROW, 0, 0, tiled=True)

    own = {0: left, 1: even_pairs(left), -1: odd_pairs(left)}
    other = swapped(left, "yh")
    oth = {0: other, 1: even_pairs(other), -1: odd_pairs(other)}
    for k in (1, 2):
        for got in (own, oth):
            got[k + 1] = even_pairs(got[-k])
            got[-k - 1] = odd_pairs(got[k])
    own[4] = even_pairs(own[-3])
    oth[4] = odd_pairs(oth[3])
    pieces, order = [], []
    for k in STEPS:
        for got, y in ((own, yh), (oth, 1 - yh)):
            spot = y * 16 + ((z + sign * k) % 8) * 2
            pieces += [got[k], swapped(got[k], "core")]
            order += [spot + core, spot + 1 - core]
    order = jnp.stack(order).astype(jnp.int32)

    high, low = turned(corner_t)

    def ring(half, one, two, flip):
        where = jnp.stack([half, core]).astype(jnp.int32)
        keep, give = row_products(where, high, low, right_full)
        got = swapped(give, "core")

        def at(k):
            spot = (z + sign * flip * k) % 8
            return lax.dynamic_index_in_dim(keep, spot, 0, keepdims=False) + (
                lax.dynamic_index_in_dim(got, spot, 0, keepdims=False)
            )

        a = one(at(4)) + at(-3)
        b = one(at(3)) + at(-2)
        a = two(a) + at(2)
        b = two(b) + at(1)
        a = one(a) + at(-1)
        b = one(b)
        a = two(a)
        return at(0), a, b

    far = ring(1 - yh, odd_pairs, even_pairs, -1)
    near = ring(yh, even_pairs, odd_pairs, 1)
    far_sum = swapped(far[0] + far[1] + far[2], "yh")
    corner_right, left_grad = total_and_product((*near, far_sum), upstream, 1, "left_gradient")

    partial_left, p_high, p_low = column_products(order, corner_t, pieces)
    blocks = partial_left.reshape(line, -1, partial_left.shape[1])
    arrived = lax.all_to_all(blocks, ROW, 0, 0, tiled=True)
    corner_left, right_grad = total_and_product((arrived,), upstream, 0, "right_gradient")

    corner_grad = corner_gradient(right_full, upstream, p_high, p_low).T
    return corner_right, corner_left, right_grad, left_grad, corner_grad


def solution(mesh):
    torus = Mesh(mesh.devices.reshape(4, 2, 2, 8, 2), ("x", "yl", "yh", "z", "core"))
    return jax.shard_map(
        body,
        mesh=torus,
        in_specs=(P(ROW, COL), P(COL, ROW), P(ROW, COL), P()),
        out_specs=(
            P(ROW + COL, None),
            P(COL + ROW, None),
            P(COL + ROW, None),
            P(ROW + COL, None),
            P(ROW, COL),
        ),
        check_vma=False,
    )
```
